32 devices in a mesh: seq: 4 (over z), head: 2 (over y), dp: 4 (over x, core).
Axes of the slice: x: 2, y: 2, z: 4, core: 2. Of those that a mesh axis runs over, the one named last changes fastest.
Arguments:
- queries: bfloat16 [8192, 8192], P(('dp', 'seq'), 'head'), parts along dimension 0, may hold values from -5 to 5
- keys: bfloat16 [8192, 1024], P(('dp', 'seq'), 'head'), parts along dimension 0, may hold values from -4 to 4
- values: bfloat16 [8192, 1024], P(('dp', 'seq'), 'head'), parts along dimension 0, may hold values from -6 to 6
- doc_lengths: int32 [32], P('dp'), parts along dimension 0, may hold values from 1 to 512, 2048 in all
- sink_rows: int32 [1024], P('dp'), parts along dimension 0, may hold values from 0 to 2047, as said below
Outputs:
- attended: bfloat16 [8192, 8192], P(('dp', 'seq'), 'head'), parts along dimension 0
The draws below stay inside these ranges and needn't reach their ends.
There are 4 independent parts, one for each index of `dp`. The reference program is written for one: setup_inputs(seed, part) draws one part's arguments, and reference() takes and returns one part's arrays. A program takes and returns all parts, laid end to end along the dimension named above; each array names one. Nothing has to cross between parts.
Inputs may be any that keep to these rules, and one draw needn't show every extreme that they name: `sink_rows`: distinct positions of the sequence. `doc_lengths`: they sum to 2048.
All inputs are finite; a program needn't handle non-finite values.
Results may differ from the reference program's by a relative error of at most 0.0046.
Values may be sent and summed in bfloat16 or wider, within the bound.
A program may use at most 64 MiB of HBM per device.

```python
import math
import jax
import jax.numpy as jnp
import numpy as np
from jax import lax

HQ = 64
KEY_VALUE_HEADS = 8
HEAD_SIZE = 128
TOKENS_PER_SHARD = 512
SINKS = 256
HALF_WIN = 1024
QUERY_PER_KV = 8
SEQUENCE_TOKENS = 2048
DOCS = 8


def draw_keys(key, part):
    sampled_rows = jnp.clip(jax.random.normal(jax.random.fold_in(key, 17), (SEQUENCE_TOKENS, KEY_VALUE_HEADS, HEAD_SIZE)), -4.0, 4.0)
    return sampled_rows.reshape(SEQUENCE_TOKENS, KEY_VALUE_HEADS * HEAD_SIZE).astype(jnp.bfloat16)


def draw_queries(key, part):
    sampled_rows = jnp.clip(jax.random.normal(jax.random.fold_in(key, 29), (SEQUENCE_TOKENS, KEY_VALUE_HEADS, QUERY_PER_KV, HEAD_SIZE)), -5.0, 5.0)
    return sampled_rows.reshape(SEQUENCE_TOKENS, HQ * HEAD_SIZE).astype(jnp.bfloat16)


def draw_sink_rows(key, part):
    early_key, late_key = jax.random.split(jax.random.fold_in(key, 23))
    quarter = SEQUENCE_TOKENS // 4
    early_count = 3 * SINKS // 4
    late_count = SINKS - early_count
    early_rows = jax.random.permutation(early_key, quarter - 1)[:early_count - 1] + 1
    late_rows = jax.random.permutation(late_key, SEQUENCE_TOKENS - quarter - 1)[:late_count - 1] + quarter
    return jnp.concatenate([jnp.zeros((1,), jnp.int32), early_rows.astype(jnp.int32), late_rows.astype(jnp.int32), jnp.full((1,), SEQUENCE_TOKENS - 1, jnp.int32)])


def shard_levels(rng, dims, pieces, low, top_value):
    def one(dim, parts):
        steps = jax.random.uniform(jax.random.fold_in(jax.random.fold_in(rng, 6), dim), (parts,), jnp.float32, low / len(pieces), top_value / len(pieces))
        return jnp.repeat(jnp.exp(steps), dims[dim] // parts).reshape((-1,) + (1,) * (len(dims) - dim - 1))

    factor_of = one(*pieces[0])
    for cut in pieces[1:]:
        factor_of = factor_of * one(*cut)
    return factor_of


def length_profile(number_of, total, bound, skew):
    loads = [(1 << 20) // math.isqrt(standing ** skew) + 1 for standing in range(2, number_of + 1)]
    spare, counts = total - bound - (number_of - 1), [1] * (number_of - 1)
    while spare > 0:
        candidates = [i for i in range(number_of - 1) if counts[i] < bound]
        whole, remaining = sum([loads[i] for i in candidates]), spare
        for i in candidates:
            more = min(bound - counts[i], max(1, remaining * loads[i] // whole), spare)
            counts[i] = counts[i] + more
            spare = spare - more
    return np.array([bound] + counts)


def ragged(key, count, total, bound, lean):
    if count == 2:
        one = jax.random.randint(key, (), max(1, total - bound), min(bound, total - 1) + 1)
        return jnp.stack([one, total - one])
    tallies = jnp.asarray(length_profile(count, total, bound, lean), jnp.int32)
    twos = (count - 1) // 2
    donor, receiver = tallies[1:1 + 2 * twos:2], tallies[2:2 + 2 * twos:2]
    margin = jnp.minimum(donor - 1, bound - receiver)
    moved = jax.random.randint(jax.random.fold_in(key, 1), (twos,), 0, 1 << 20) % (margin + 1)
    tallies = tallies.at[1:1 + 2 * twos:2].set(donor - moved).at[2:2 + 2 * twos:2].set(receiver + moved)
    return tallies[jax.random.permutation(jax.random.fold_in(key, 2), count)]


def normal_values(rng, shape, scale, most, pieces=(), kind=jnp.bfloat16):
    factor_of = shard_levels(rng, shape, pieces, -0.22, 0.18) if pieces else 1.0
    entries = jax.random.normal(rng, shape, jnp.float32) * scale * factor_of
    return jnp.minimum(jnp.maximum(entries, -most), most).astype(kind)


def setup_inputs(seed: int = 0, part: int = 0) -> dict:
    key_of = jax.random.split(jax.random.key(seed), 6)
    part_keys = jax.random.split(jax.random.fold_in(key_of[5], part), 6)
    return {
        "queries": draw_queries(jax.random.fold_in(jax.random.fold_in(key_of[5], part), 71), part),
        "keys": draw_keys(jax.random.fold_in(jax.random.fold_in(key_of[5], part), 71), part),
        "values": normal_values(part_keys[2], (SEQUENCE_TOKENS, KEY_VALUE_HEADS * HEAD_SIZE), 1.0, 6.0, ((0, 4), (1, 2))),
        "doc_lengths": ragged(part_keys[3], DOCS, SEQUENCE_TOKENS, SEQUENCE_TOKENS // 4, 1).astype(jnp.int32),
        "sink_rows": draw_sink_rows(jax.random.fold_in(jax.random.fold_in(key_of[5], part), 71), part),
    }


def document_ids(positions, starts):
    return lax.optimization_barrier(jnp.sum((starts[None, :] <= positions[:, None]).astype(jnp.int32), axis=1))

def reference(queries, keys, values, doc_lengths, sink_rows):
    seq_len = queries.shape[0]
    starts = (jnp.cumsum(doc_lengths) - doc_lengths).astype(jnp.int32)
    all_pos = jnp.arange(seq_len, dtype=jnp.int32)
    all_docs = document_ids(all_pos, starts)
    sink_flag = jnp.zeros((seq_len,), jnp.int32).at[sink_rows].set(1)
    global_sink_keys = keys[sink_rows]
    global_sink_values = values[sink_rows]
    pad_keys = jnp.pad(keys, ((HALF_WIN, HALF_WIN), (0, 0)))
    pad_values = jnp.pad(values, ((HALF_WIN, HALF_WIN), (0, 0)))
    pad_docs = jnp.pad(all_docs, (HALF_WIN, HALF_WIN), constant_values=-1)
    pad_flags = jnp.pad(sink_flag, (HALF_WIN, HALF_WIN))
    key_span = TOKENS_PER_SHARD + 2 * HALF_WIN
    score_scale = 1.0 / math.sqrt(HEAD_SIZE)

    def one_block(block_index):
        leading_row = (block_index * TOKENS_PER_SHARD).astype(jnp.int32)
        local_window_keys = lax.dynamic_slice_in_dim(pad_keys, leading_row, key_span, 0)
        local_window_values = lax.dynamic_slice_in_dim(pad_values, leading_row, key_span, 0)
        window_docs = lax.dynamic_slice_in_dim(pad_docs, leading_row, key_span, 0)
        window_flags = lax.dynamic_slice_in_dim(pad_flags, leading_row, key_span, 0)
        key_pos = leading_row - HALF_WIN + jnp.arange(key_span, dtype=jnp.int32)
        query_pos = leading_row + jnp.arange(TOKENS_PER_SHARD, dtype=jnp.int32)
        query_docs = lax.dynamic_slice_in_dim(all_docs, leading_row, TOKENS_PER_SHARD, 0)
        window_ok = (jnp.abs(query_pos[:, None] - key_pos[None, :]) <= HALF_WIN) & (query_docs[:, None] == window_docs[None, :]) & (window_flags[None, :] == 0)
        visible = jnp.concatenate([window_ok, jnp.ones((TOKENS_PER_SHARD, SINKS), jnp.bool_)], axis=1)
        complete_keys = jnp.concatenate([local_window_keys, global_sink_keys], axis=0).reshape(-1, KEY_VALUE_HEADS, HEAD_SIZE).astype(jnp.float32)
        complete_values = jnp.concatenate([local_window_values, global_sink_values], axis=0).reshape(-1, KEY_VALUE_HEADS, HEAD_SIZE).astype(jnp.float32)
        query_block = lax.dynamic_slice_in_dim(queries, leading_row, TOKENS_PER_SHARD, 0).reshape(TOKENS_PER_SHARD, KEY_VALUE_HEADS, QUERY_PER_KV, HEAD_SIZE).astype(jnp.float32)
        scores = jnp.einsum('bhgd,lhd->hgbl', query_block, complete_keys) * score_scale
        scores = jnp.where(visible[None, None], scores, -jnp.inf)
        row_max = lax.optimization_barrier(jnp.max(scores, axis=-1, keepdims=True))
        exp_scores = jnp.exp(scores - row_max)
        row_total = lax.optimization_barrier(jnp.sum(exp_scores, axis=-1))
        weights = lax.optimization_barrier(exp_scores.astype(jnp.bfloat16)).astype(jnp.float32)
        summed = jnp.einsum('hgbl,lhd->bhgd', weights, complete_values)
        result = summed / jnp.transpose(row_total, (2, 0, 1))[..., None]
        return result.astype(jnp.bfloat16).reshape(TOKENS_PER_SHARD, HQ * HEAD_SIZE)
    blocks = lax.map(one_block, jnp.arange(seq_len // TOKENS_PER_SHARD, dtype=jnp.int32))
    return blocks.reshape(seq_len, HQ * HEAD_SIZE)
```

```python
import functools
import math

import jax
import jax.numpy as jnp
from jax import lax
from jax.experimental import pallas as pl
from jax.experimental.pallas import tpu as pltpu
from jax.sharding import PartitionSpec as P

HEAD_SIZE = 128
HALF_WIN = 1024
CHAIN = 4
CHUNK = 256
TILE = 128
HIDE = -1e30
EXP2_SCALE = math.log2(math.e) / math.sqrt(HEAD_SIZE)
MESH = pl.DeviceIdType.MESH


def exchange_kernel(
    n, hops, k_ref, v_ref, sink_ref, nk_ref, nv_ref, sk_ref, sv_ref,
    mine, up_in, up_out, dn_in, dn_out,
    nk_send, nk_recv, nv_send, nv_recv, up_send, up_recv, dn_send, dn_recv,
):
    me = lax.axis_index("seq")
    tok, width = k_ref.shape
    sinks = sink_ref.shape[0]
    part = sinks // CHAIN

    def has(shift):
        return me + shift < n if shift > 0 else me + shift >= 0

    shifts = [d for h in range(1, hops + 1) for d in (h, -h)]
    barrier = pltpu.get_barrier_semaphore()
    for d in shifts:
        @pl.when(has(d))
        def _():
            pl.semaphore_signal(barrier, inc=1, device_id={"seq": me + d}, device_id_type=MESH)
    pl.semaphore_wait(barrier, sum(has(d).astype(jnp.int32) for d in shifts))

    def block_copies(d):
        i = shifts.index(d)
        slot = hops - d if d > 0 else hops - 1 - d
        return [
            pltpu.make_async_remote_copy(
                src_ref=src, dst_ref=dst.at[slot], send_sem=ss.at[i], recv_sem=rs.at[i],
                device_id={"seq": me + d}, device_id_type=MESH,
            )
            for src, dst, ss, rs in (
                (k_ref, nk_ref, nk_send, nk_recv), (v_ref, nv_ref, nv_send, nv_recv)
            )
        ]

    def chain_copy(c, d):
        src, dst, ss, rs = (
            (up_out, up_in, up_send, up_recv) if d > 0 else (dn_out, dn_in, dn_send, dn_recv)
        )
        rows = pl.ds(c * part, part)
        return pltpu.make_async_remote_copy(
            src_ref=src.at[rows], dst_ref=dst.at[rows], send_sem=ss.at[c], recv_sem=rs.at[c],
            device_id={"seq": me + d}, device_id_type=MESH,
        )

    pos = me * tok + lax.broadcasted_iota(jnp.int32, (sinks, tok), 1)
    pick = (sink_ref[...] == pos).astype(jnp.bfloat16)
    mine[:, :width] = jnp.dot(pick, k_ref[...], preferred_element_type=jnp.float32).astype(jnp.bfloat16)
    mine[:, width:] = jnp.dot(pick, v_ref[...], preferred_element_type=jnp.float32).astype(jnp.bfloat16)

    for d, out in ((1, up_out), (-1, dn_out)):
        @pl.when(jnp.logical_not(has(-d)))
        def _():
            out[...] = mine[...]
            for c in range(CHAIN):
                chain_copy(c, d).start()
    for d in shifts:
        @pl.when(has(d))
        def _():
            for copy in block_copies(d):
                copy.start()
    for c in range(CHAIN):
        rows = pl.ds(c * part, part)
        for d, got, out in ((1, up_in, up_out), (-1, dn_in, dn_out)):
            @pl.when(has(d) & has(-d))
            def _():
                chain_copy(c, d).wait_recv()
                out[rows, :] = mine[rows, :] + got[rows, :]
                chain_copy(c, d).start()
    @pl.when(has(1) & has(-1))
    def _():
        both = mine[...] + up_in[...] + dn_in[...]
        sk_ref[...] = both[:, :width]
        sv_ref[...] = both[:, width:]

    @pl.when(jnp.logical_not(has(-1)))
    def _():
        for c in range(CHAIN):
            chain_copy(c, -1).wait_recv()
        both = mine[...] + dn_in[...]
        sk_ref[...] = both[:, :width]
        sv_ref[...] = both[:, width:]

    @pl.when(jnp.logical_not(has(1)))
    def _():
        for c in range(CHAIN):
            chain_copy(c, 1).wait_recv()
        both = mine[...] + up_in[...]
        sk_ref[...] = both[:, :width]
        sv_ref[...] = both[:, width:]

    for d in (1, -1):
        @pl.when(has(d))
        def _():
            for c in range(CHAIN):
                chain_copy(c, d).wait_send()
    for d in shifts:
        @pl.when(has(d))
        def _():
            for copy in block_copies(d):
                copy.wait_send()

        @pl.when(has(-d))
        def _():
            for copy in block_copies(d):
                copy.wait_recv()


def attend_kernel(
    group, hops, span_ref, q_ref, k_ref, v_ref, nk_ref, nv_ref, sk_ref, sv_ref, qa_ref, ka_ref,
    o_ref, all_k, all_v, query, acc, sem,
):
    head, tile = pl.program_id(0), pl.program_id(1)
    tok = k_ref.shape[0]
    rows = q_ref.shape[0]
    dim = HEAD_SIZE
    blocks = [(nk_ref.at[j], nv_ref.at[j], j) for j in range(hops)]
    blocks += [(k_ref, v_ref, hops)]
    blocks += [(nk_ref.at[j], nv_ref.at[j], j + 1) for j in range(hops, 2 * hops)]

    @pl.when(tile == 0)
    def _():
        cols = pl.ds(pl.multiple_of(head * dim, dim), dim)
        copies = []
        for ks, vs, b in blocks:
            to = pl.ds(b * tok, tok)
            copies.append(pltpu.make_async_copy(ks.at[:, cols], all_k.at[to], sem.at[0, b]))
            copies.append(pltpu.make_async_copy(vs.at[:, cols], all_v.at[to], sem.at[1, b]))
        for copy in copies:
            copy.start()
        for copy in copies:
            copy.wait()

    for g in range(group):
        query[g * rows : (g + 1) * rows, :dim] = q_ref[:, g * dim : (g + 1) * dim]
        query[g * rows : (g + 1) * rows, dim:] = qa_ref[...]

    first, last = span_ref[2 * tile], span_ref[2 * tile + 1]
    sinks = sk_ref.shape[0]
    contract = (((1,), (1,)), ((), ()))

    def sink_scores():
        return lax.dot_general(query[:, :dim], sk_ref[...], contract, preferred_element_type=jnp.float32)

    def chunk_scores(c):
        at = pl.ds(pl.multiple_of(c * CHUNK, CHUNK), CHUNK)
        keys = jnp.concatenate([all_k[at, :], ka_ref[at, :]], axis=1)
        scores = lax.dot_general(query[...], keys, contract, preferred_element_type=jnp.float32)
        if hops > 1:
            i = lax.broadcasted_iota(jnp.int32, (rows, CHUNK), 0) + tile * rows
            j = lax.broadcasted_iota(jnp.int32, (rows, CHUNK), 1) + c * CHUNK - hops * tok
            near = jnp.where(jnp.abs(i - j) <= HALF_WIN, 0.0, HIDE)
            scores = scores + jnp.concatenate([near] * group, axis=0)
        return scores

    def with_ones(values):
        return jnp.concatenate([values, jnp.ones(values.shape, values.dtype)], axis=1)

    def chunk_values(c):
        at = pl.ds(pl.multiple_of(c * CHUNK, CHUNK), CHUNK)
        return with_ones(all_v[at, :])

    def accumulate(weigh):
        acc[...] = jnp.dot(weigh(sink_scores()), with_ones(sv_ref[...]), preferred_element_type=jnp.float32)

        @pl.loop(first, last)
        def _(c):
            acc[...] += jnp.dot(weigh(chunk_scores(c)), chunk_values(c), preferred_element_type=jnp.float32)

    accumulate(lambda s: jnp.exp2(s * EXP2_SCALE).astype(jnp.bfloat16))
    total = acc[:, dim:]
    in_range = (jnp.min(total) >= 2.0**-60) & (jnp.max(total) <= 2.0**100)

    @pl.when(jnp.logical_not(in_range))
    def _():
        top = jnp.max(sink_scores(), axis=1, keepdims=True)
        top = lax.fori_loop(
            first, last,
            lambda c, m: jnp.maximum(m, jnp.max(chunk_scores(c), axis=1, keepdims=True)),
            top,
        )
        accumulate(lambda s: jnp.exp2((s - top) * EXP2_SCALE).astype(jnp.bfloat16))

    for g in range(group):
        part = acc[g * rows : (g + 1) * rows, :]
        o_ref[:, g * dim : (g + 1) * dim] = (part[:, :dim] / part[:, dim:]).astype(o_ref.dtype)


def on_device(n, queries, keys, values, doc_lengths, sink_rows):
    tok, width = keys.shape
    dim = HEAD_SIZE
    kv_heads = width // dim
    group = queries.shape[1] // width
    seq_len = tok * n
    sinks = sink_rows.shape[0]
    docs = doc_lengths.shape[0]
    longest = seq_len // 4
    hops = min(-(-min(HALF_WIN, longest - 1) // tok), n - 1)
    span = (2 * hops + 1) * tok
    any_space = pl.BlockSpec(memory_space=pl.ANY)
    vmem = pl.BlockSpec(memory_space=pltpu.VMEM)
    bf16 = jnp.bfloat16
    dma = pltpu.SemaphoreType.DMA

    near_k, near_v, sink_k, sink_v = pl.pallas_call(
        functools.partial(exchange_kernel, n, hops),
        out_shape=[
            jax.ShapeDtypeStruct((2 * hops, tok, width), bf16),
            jax.ShapeDtypeStruct((2 * hops, tok, width), bf16),
            jax.ShapeDtypeStruct((sinks, width), bf16),
            jax.ShapeDtypeStruct((sinks, width), bf16),
        ],
        in_specs=[vmem, vmem, vmem],
        out_specs=[any_space, any_space, vmem, vmem],
        scratch_shapes=[pltpu.VMEM((sinks, 2 * width), bf16)] * 5
        + [dma((2 * hops,))] * 4 + [dma((CHAIN,))] * 4,
        compiler_params=pltpu.CompilerParams(
            collective_id=0, has_side_effects=True, vmem_limit_bytes=32 << 20
        ),
        name="exchange",
    )(keys, values, sink_rows.reshape(sinks, 1))

    first_row = lax.axis_index("seq") * tok
    base = first_row - hops * tok
    ends = jnp.cumsum(doc_lengths)
    starts = ends - doc_lengths

    def member(p):
        lane_s = jnp.pad(starts, (0, dim - docs), constant_values=seq_len)
        lane_e = jnp.pad(ends, (0, dim - docs), constant_values=seq_len)
        return (p[:, None] >= lane_s[None, :]) & (p[:, None] < lane_e[None, :])

    q_pos = first_row + jnp.arange(tok, dtype=jnp.int32)
    k_pos = base + jnp.arange(span, dtype=jnp.int32)
    q_side = member(q_pos).astype(bf16)
    is_sink = jnp.any(k_pos[:, None] == sink_rows[None, :], axis=1)
    k_side = jnp.where(member(k_pos) & jnp.logical_not(is_sink)[:, None], 0.0, HIDE).astype(bf16)
    a = first_row + jnp.arange(0, tok, TILE, dtype=jnp.int32)
    b = a + TILE
    low = jnp.max(jnp.where(starts[None, :] <= a[:, None], starts[None, :], 0), axis=1)
    high = jnp.min(jnp.where(ends[None, :] >= b[:, None], ends[None, :], seq_len), axis=1)
    low = jnp.maximum(jnp.maximum(low, a - HALF_WIN), jnp.maximum(base, 0)) - base
    high = jnp.minimum(jnp.minimum(high, b + HALF_WIN), jnp.minimum(base + span, seq_len)) - base
    spans = jnp.stack([low // CHUNK, (high + CHUNK - 1) // CHUNK], axis=1).reshape(-1).astype(jnp.int32)

    return pl.pallas_call(
        functools.partial(attend_kernel, group, hops),
        out_shape=jax.ShapeDtypeStruct(queries.shape, queries.dtype),
        grid_spec=pltpu.PrefetchScalarGridSpec(
            num_scalar_prefetch=1,
            grid=(kv_heads, tok // TILE),
            in_specs=[
                pl.BlockSpec((TILE, group * dim), lambda h, t, s: (t, h)),
                any_space, any_space, any_space, any_space,
                pl.BlockSpec((sinks, dim), lambda h, t, s: (0, h)),
                pl.BlockSpec((sinks, dim), lambda h, t, s: (0, h)),
                pl.BlockSpec((TILE, dim), lambda h, t, s: (t, 0)),
                pl.BlockSpec((span, dim), lambda h, t, s: (0, 0)),
            ],
            out_specs=pl.BlockSpec((TILE, group * dim), lambda h, t, s: (t, h)),
            scratch_shapes=[
                pltpu.VMEM((span, dim), bf16),
                pltpu.VMEM((span, dim), bf16),
                pltpu.VMEM((TILE * group, 2 * dim), bf16),
                pltpu.VMEM((TILE * group, 2 * dim), jnp.float32),
                dma((2, 2 * hops + 1)),
            ],
        ),
        compiler_params=pltpu.CompilerParams(vmem_limit_bytes=40 << 20),
        name="attend",
    )(spans, queries, keys, values, near_k, near_v, sink_k, sink_v, q_side, k_side)


def solution(mesh):
    return jax.shard_map(
        functools.partial(on_device, mesh.shape["seq"]),
        mesh=mesh,
        in_specs=(
            P(("dp", "seq"), "head"),
            P(("dp", "seq"), "head"),
            P(("dp", "seq"), "head"),
            P("dp"),
            P("dp"),
        ),
        out_specs=P(("dp", "seq"), "head"),
        check_vma=False,
    )
```

```python
import functools
import math

import jax
import jax.numpy as jnp
from jax import lax
from jax.experimental import pallas as pl
from jax.experimental.pallas import tpu as pltpu
from jax.sharding import PartitionSpec as P

HEAD_SIZE = 128
HALF_WIN = 1024
CHAIN = 4
CHUNK = 256
TILE = 256
HIDE = -1e30
EXP2_SCALE = math.log2(math.e) / math.sqrt(HEAD_SIZE)
MESH = pl.DeviceIdType.MESH


def exchange_kernel(
    n, hops, k_ref, v_ref, sink_ref, nk_ref, nv_ref, sk_ref, sv_ref,
    mine, up_in, up_out, dn_in, dn_out,
    nk_send, nk_recv, nv_send, nv_recv, up_send, up_recv, dn_send, dn_recv, own_sem,
):
    me = lax.axis_index("seq")
    tok, width = k_ref.shape
    sinks = sink_ref.shape[0]
    part = sinks // CHAIN

    def has(shift):
        return me + shift < n if shift > 0 else me + shift >= 0

    shifts = [d for h in range(1, hops + 1) for d in (h, -h)]
    barrier = pltpu.get_barrier_semaphore()
    for d in shifts:
        @pl.when(has(d))
        def _():
            pl.semaphore_signal(barrier, inc=1, device_id={"seq": me + d}, device_id_type=MESH)
    pl.semaphore_wait(barrier, sum(has(d).astype(jnp.int32) for d in shifts))

    def block_copies(d):
        i = shifts.index(d)
        place = pl.ds((hops - d) * tok, tok)
        return [
            pltpu.make_async_remote_copy(
                src_ref=src, dst_ref=dst.at[place], send_sem=ss.at[i], recv_sem=rs.at[i],
                device_id={"seq": me + d}, device_id_type=MESH,
            )
            for src, dst, ss, rs in (
                (k_ref, nk_ref, nk_send, nk_recv), (v_ref, nv_ref, nv_send, nv_recv)
            )
        ]

    def chain_copy(c, d):
        src, dst, ss, rs = (
            (up_out, up_in, up_send, up_recv) if d > 0 else (dn_out, dn_in, dn_send, dn_recv)
        )
        rows = pl.ds(pl.multiple_of(c * part, part), part)
        return pltpu.make_async_remote_copy(
            src_ref=src.at[rows], dst_ref=dst.at[rows], send_sem=ss.at[c], recv_sem=rs.at[c],
            device_id={"seq": me + d}, device_id_type=MESH,
        )

    own = pl.ds(hops * tok, tok)
    keep = [
        pltpu.make_async_copy(k_ref, nk_ref.at[own], own_sem.at[0]),
        pltpu.make_async_copy(v_ref, nv_ref.at[own], own_sem.at[1]),
    ]
    for copy in keep:
        copy.start()

    pos = me * tok + lax.broadcasted_iota(jnp.int32, (sinks, tok), 1)
    pick = (sink_ref[...] == pos).astype(jnp.bfloat16)
    mine[:, :width] = jnp.dot(pick, k_ref[...], preferred_element_type=jnp.float32).astype(jnp.bfloat16)
    mine[:, width:] = jnp.dot(pick, v_ref[...], preferred_element_type=jnp.float32).astype(jnp.bfloat16)

    for d, out in ((1, up_out), (-1, dn_out)):
        @pl.when(jnp.logical_not(has(-d)))
        def _():
            out[...] = mine[...]
            for c in range(CHAIN):
                chain_copy(c, d).start()
    for d in shifts:
        @pl.when(has(d))
        def _():
            for copy in block_copies(d):
                copy.start()
    for step in range(n - 1 + CHAIN):
        for d, got, out, hop in ((1, up_in, up_out, me), (-1, dn_in, dn_out, n - 1 - me)):
            c = step - hop

            @pl.when(has(-d) & (c >= 0) & (c < CHAIN))
            def _():
                chain_copy(c, d).wait_recv()

            @pl.when(has(d) & has(-d) & (c >= 0) & (c < CHAIN))
            def _():
                rows = pl.ds(pl.multiple_of(c * part, part), part)
                out[rows, :] = mine[rows, :] + got[rows, :]
                chain_copy(c, d).start()

    @pl.when(has(1) & has(-1))
    def _():
        both = mine[...] + up_in[...] + dn_in[...]
        sk_ref[...] = both[:, :width]
        sv_ref[...] = both[:, width:]

    @pl.when(jnp.logical_not(has(-1)))
    def _():
        both = mine[...] + dn_in[...]
        sk_ref[...] = both[:, :width]
        sv_ref[...] = both[:, width:]

    @pl.when(jnp.logical_not(has(1)))
    def _():
        both = mine[...] + up_in[...]
        sk_ref[...] = both[:, :width]
        sv_ref[...] = both[:, width:]

    for d in (1, -1):
        @pl.when(has(d))
        def _():
            for c in range(CHAIN):
                chain_copy(c, d).wait_send()
    for d in shifts:
        @pl.when(has(d))
        def _():
            for copy in block_copies(d):
                copy.wait_send()

        @pl.when(has(-d))
        def _():
            for copy in block_copies(d):
                copy.wait_recv()
    for copy in keep:
        copy.wait()


def attend_kernel(
    group, hops, span_ref, q_ref, all_k, all_v, sk_ref, sv_ref, qa_ref, ka_ref,
    o_ref, query, acc,
):
    tile = pl.program_id(1)
    tok = all_k.shape[0] // (2 * hops + 1)
    rows = q_ref.shape[0]
    dim = HEAD_SIZE
    for g in range(group):
        query[g * rows : (g + 1) * rows, :dim] = q_ref[:, g * dim : (g + 1) * dim]
        query[g * rows : (g + 1) * rows, dim:] = qa_ref[...]

    first, last = span_ref[2 * tile], span_ref[2 * tile + 1]
    sinks = sk_ref.shape[0]
    contract = (((1,), (1,)), ((), ()))

    def sink_scores():
        return lax.dot_general(query[:, :dim], sk_ref[...], contract, preferred_element_type=jnp.float32)

    def chunk_scores(c):
        at = pl.ds(pl.multiple_of(c * CHUNK, CHUNK), CHUNK)
        keys = jnp.concatenate([all_k[at, :], ka_ref[at, :]], axis=1)
        scores = lax.dot_general(query[...], keys, contract, preferred_element_type=jnp.float32)
        if hops > 1:
            i = lax.broadcasted_iota(jnp.int32, (rows, CHUNK), 0) + tile * rows
            j = lax.broadcasted_iota(jnp.int32, (rows, CHUNK), 1) + c * CHUNK - hops * tok
            near = jnp.where(jnp.abs(i - j) <= HALF_WIN, 0.0, HIDE)
            scores = scores + jnp.concatenate([near] * group, axis=0)
        return scores

    def with_ones(values):
        return jnp.concatenate([values, jnp.ones(values.shape, values.dtype)], axis=1)

    def chunk_values(c):
        at = pl.ds(pl.multiple_of(c * CHUNK, CHUNK), CHUNK)
        return with_ones(all_v[at, :])

    def accumulate(weigh):
        acc[...] = jnp.dot(weigh(sink_scores()), with_ones(sv_ref[...]), preferred_element_type=jnp.float32)

        @pl.loop(first, last)
        def _(c):
            acc[...] += jnp.dot(weigh(chunk_scores(c)), chunk_values(c), preferred_element_type=jnp.float32)

    accumulate(lambda s: jnp.exp2(s * EXP2_SCALE).astype(jnp.bfloat16))
    total = acc[:, dim:]
    in_range = (jnp.min(total) >= 2.0**-60) & (jnp.max(total) <= 2.0**100)

    @pl.when(jnp.logical_not(in_range))
    def _():
        top = jnp.max(sink_scores(), axis=1, keepdims=True)
        top = lax.fori_loop(
            first, last,
            lambda c, m: jnp.maximum(m, jnp.max(chunk_scores(c), axis=1, keepdims=True)),
            top,
        )
        accumulate(lambda s: jnp.exp2((s - top) * EXP2_SCALE).astype(jnp.bfloat16))

    for g in range(group):
        part = acc[g * rows : (g + 1) * rows, :]
        o_ref[:, g * dim : (g + 1) * dim] = (part[:, :dim] / part[:, dim:]).astype(o_ref.dtype)


def on_device(n, queries, keys, values, doc_lengths, sink_rows):
    tok, width = keys.shape
    dim = HEAD_SIZE
    kv_heads = width // dim
    group = queries.shape[1] // width
    seq_len = tok * n
    sinks = sink_rows.shape[0]
    docs = doc_lengths.shape[0]
    longest = seq_len // 4
    hops = min(-(-min(HALF_WIN, longest - 1) // tok), n - 1)
    span = (2 * hops + 1) * tok
    any_space = pl.BlockSpec(memory_space=pl.ANY)
    vmem = pl.BlockSpec(memory_space=pltpu.VMEM)
    bf16 = jnp.bfloat16
    dma = pltpu.SemaphoreType.DMA

    near_k, near_v, sink_k, sink_v = pl.pallas_call(
        functools.partial(exchange_kernel, n, hops),
        out_shape=[
            jax.ShapeDtypeStruct((span, width), bf16),
            jax.ShapeDtypeStruct((span, width), bf16),
            jax.ShapeDtypeStruct((sinks, width), bf16),
            jax.ShapeDtypeStruct((sinks, width), bf16),
        ],
        in_specs=[vmem, vmem, vmem],
        out_specs=[any_space, any_space, vmem, vmem],
        scratch_shapes=[pltpu.VMEM((sinks, 2 * width), bf16)] * 5
        + [dma((2 * hops,))] * 4 + [dma((CHAIN,))] * 4 + [dma((2,))],
        compiler_params=pltpu.CompilerParams(
            collective_id=0, has_side_effects=True, vmem_limit_bytes=32 << 20
        ),
        name="exchange",
    )(keys, values, sink_rows.reshape(sinks, 1))

    first_row = lax.axis_index("seq") * tok
    base = first_row - hops * tok
    ends = jnp.cumsum(doc_lengths)
    starts = ends - doc_lengths

    def member(p):
        lane_s = jnp.pad(starts, (0, dim - docs), constant_values=seq_len)
        lane_e = jnp.pad(ends, (0, dim - docs), constant_values=seq_len)
        return (p[:, None] >= lane_s[None, :]) & (p[:, None] < lane_e[None, :])

    q_pos = first_row + jnp.arange(tok, dtype=jnp.int32)
    k_pos = base + jnp.arange(span, dtype=jnp.int32)
    q_side = member(q_pos).astype(bf16)
    is_sink = jnp.any(k_pos[:, None] == sink_rows[None, :], axis=1)
    k_side = jnp.where(member(k_pos) & jnp.logical_not(is_sink)[:, None], 0.0, HIDE).astype(bf16)
    a = first_row + jnp.arange(0, tok, TILE, dtype=jnp.int32)
    b = a + TILE
    low = jnp.max(jnp.where(starts[None, :] <= a[:, None], starts[None, :], 0), axis=1)
    high = jnp.min(jnp.where(ends[None, :] >= b[:, None], ends[None, :], seq_len), axis=1)
    low = jnp.maximum(jnp.maximum(low, a - HALF_WIN), jnp.maximum(base, 0)) - base
    high = jnp.minimum(jnp.minimum(high, b + HALF_WIN), jnp.minimum(base + span, seq_len)) - base
    spans = jnp.stack([low // CHUNK, (high + CHUNK - 1) // CHUNK], axis=1).reshape(-1).astype(jnp.int32)

    return pl.pallas_call(
        functools.partial(attend_kernel, group, hops),
        out_shape=jax.ShapeDtypeStruct(queries.shape, queries.dtype),
        grid_spec=pltpu.PrefetchScalarGridSpec(
            num_scalar_prefetch=1,
            grid=(kv_heads, tok // TILE),
            in_specs=[
                pl.BlockSpec((TILE, group * dim), lambda h, t, s: (t, h)),
                pl.BlockSpec((span, dim), lambda h, t, s: (0, h)),
                pl.BlockSpec((span, dim), lambda h, t, s: (0, h)),
                pl.BlockSpec((sinks, dim), lambda h, t, s: (0, h)),
                pl.BlockSpec((sinks, dim), lambda h, t, s: (0, h)),
                pl.BlockSpec((TILE, dim), lambda h, t, s: (t, 0)),
                pl.BlockSpec((span, dim), lambda h, t, s: (0, 0)),
            ],
            out_specs=pl.BlockSpec((TILE, group * dim), lambda h, t, s: (t, h)),
            scratch_shapes=[
                pltpu.VMEM((TILE * group, 2 * dim), bf16),
                pltpu.VMEM((TILE * group, 2 * dim), jnp.float32),
            ],
        ),
        compiler_params=pltpu.CompilerParams(vmem_limit_bytes=40 << 20),
        name="attend",
    )(spans, queries, near_k, near_v, sink_k, sink_v, q_side, k_side)


def solution(mesh):
    return jax.shard_map(
        functools.partial(on_device, mesh.shape["seq"]),
        mesh=mesh,
        in_specs=(
            P(("dp", "seq"), "head"),
            P(("dp", "seq"), "head"),
            P(("dp", "seq"), "head"),
            P("dp"),
            P("dp"),
        ),
        out_specs=P(("dp", "seq"), "head"),
        check_vma=False,
    )
```

```python
import functools
import math

import jax
import jax.numpy as jnp
from jax import lax
from jax.experimental import pallas as pl
from jax.experimental.pallas import tpu as pltpu
from jax.sharding import PartitionSpec as P

HEAD_SIZE = 128
HALF_WIN = 1024
CHAIN = 4
CHUNK = 256
TILE = 256
HIDE = -1e30
EXP2_SCALE = math.log2(math.e) / math.sqrt(HEAD_SIZE)
MESH = pl.DeviceIdType.MESH


def exchange_kernel(
    n, hops, k_ref, v_ref, sink_ref, lane_ref, docs_ref, nk_ref, nv_ref, sk_ref, sv_ref, qa_ref, ka_ref,
    mine, up_in, up_out, dn_in, dn_out,
    nk_send, nk_recv, nv_send, nv_recv, up_send, up_recv, dn_send, dn_recv, own_sem,
):
    me = lax.axis_index("seq")
    tok, width = k_ref.shape
    sinks = sink_ref.shape[0]
    part = sinks // CHAIN

    def has(shift):
        return me + shift < n if shift > 0 else me + shift >= 0

    shifts = [d for h in range(1, hops + 1) for d in (h, -h)]
    barrier = pltpu.get_barrier_semaphore()
    for d in shifts:
        @pl.when(has(d))
        def _():
            pl.semaphore_signal(barrier, inc=1, device_id={"seq": me + d}, device_id_type=MESH)
    pl.semaphore_wait(barrier, sum(has(d).astype(jnp.int32) for d in shifts))

    def block_copies(d):
        i = shifts.index(d)
        place = pl.ds((hops - d) * tok, tok)
        return [
            pltpu.make_async_remote_copy(
                src_ref=src, dst_ref=dst.at[place], send_sem=ss.at[i], recv_sem=rs.at[i],
                device_id={"seq": me + d}, device_id_type=MESH,
            )
            for src, dst, ss, rs in (
                (k_ref, nk_ref, nk_send, nk_recv), (v_ref, nv_ref, nv_send, nv_recv)
            )
        ]

    def chain_copy(c, d):
        src, dst, ss, rs = (
            (up_out, up_in, up_send, up_recv) if d > 0 else (dn_out, dn_in, dn_send, dn_recv)
        )
        rows = pl.ds(pl.multiple_of(c * part, part), part)
        return pltpu.make_async_remote_copy(
            src_ref=src.at[rows], dst_ref=dst.at[rows], send_sem=ss.at[c], recv_sem=rs.at[c],
            device_id={"seq": me + d}, device_id_type=MESH,
        )

    own = pl.ds(hops * tok, tok)
    keep = [
        pltpu.make_async_copy(k_ref, nk_ref.at[own], own_sem.at[0]),
        pltpu.make_async_copy(v_ref, nv_ref.at[own], own_sem.at[1]),
    ]
    for copy in keep:
        copy.start()

    pos = me * tok + lax.broadcasted_iota(jnp.int32, (sinks, tok), 1)
    pick = (sink_ref[...] == pos).astype(jnp.bfloat16)
    mine[:, :width] = jnp.dot(pick, k_ref[...], preferred_element_type=jnp.float32).astype(jnp.bfloat16)
    mine[:, width:] = jnp.dot(pick, v_ref[...], preferred_element_type=jnp.float32).astype(jnp.bfloat16)

    for d, out in ((1, up_out), (-1, dn_out)):
        @pl.when(jnp.logical_not(has(-d)))
        def _():
            out[...] = mine[...]
            for c in range(CHAIN):
                chain_copy(c, d).start()
    for d in shifts:
        @pl.when(has(d))
        def _():
            for copy in block_copies(d):
                copy.start()
    docs = docs_ref.shape[0]
    d_row = lax.broadcasted_iota(jnp.int32, (docs, HEAD_SIZE), 0)
    d_lane = lax.broadcasted_iota(jnp.int32, (docs, HEAD_SIZE), 1)
    starts = jnp.sum(jnp.where(d_row < d_lane, docs_ref[...], 0), axis=0, keepdims=True)
    ends = jnp.sum(jnp.where(d_row <= d_lane, docs_ref[...], 0), axis=0, keepdims=True)

    def member(first):
        p = first + lax.broadcasted_iota(jnp.int32, (tok, HEAD_SIZE), 0)
        return (p >= starts) & (p < ends)

    def query_side():
        qa_ref[...] = jnp.where(member(me * tok), 1.0, 0.0).astype(jnp.bfloat16)

    def key_side(block):
        first = (me + block - hops) * tok
        p = first + lax.broadcasted_iota(jnp.int32, (tok, sinks), 0)
        found = jnp.max(jnp.where(p == lane_ref[...], 1, 0), axis=1, keepdims=True)
        seen = member(first) & (found == 0)
        ka_ref[block * tok : (block + 1) * tok, :] = jnp.where(seen, 0.0, HIDE).astype(jnp.bfloat16)

    sides = [query_side] + [functools.partial(key_side, b) for b in range(2 * hops + 1)]

    for step in range(n - 1 + CHAIN):
        for d, got, out, hop in ((1, up_in, up_out, me), (-1, dn_in, dn_out, n - 1 - me)):
            c = step - hop

            @pl.when(has(-d) & (c >= 0) & (c < CHAIN))
            def _():
                chain_copy(c, d).wait_recv()

            @pl.when(has(d) & has(-d) & (c >= 0) & (c < CHAIN))
            def _():
                rows = pl.ds(pl.multiple_of(c * part, part), part)
                out[rows, :] = mine[rows, :] + got[rows, :]
                chain_copy(c, d).start()
        if sides:
            sides.pop()()
    while sides:
        sides.pop()()

    @pl.when(has(1) & has(-1))
    def _():
        both = mine[...] + up_in[...] + dn_in[...]
        sk_ref[...] = both[:, :width]
        sv_ref[...] = both[:, width:]

    @pl.when(jnp.logical_not(has(-1)))
    def _():
        both = mine[...] + dn_in[...]
        sk_ref[...] = both[:, :width]
        sv_ref[...] = both[:, width:]

    @pl.when(jnp.logical_not(has(1)))
    def _():
        both = mine[...] + up_in[...]
        sk_ref[...] = both[:, :width]
        sv_ref[...] = both[:, width:]

    for d in (1, -1):
        @pl.when(has(d))
        def _():
            for c in range(CHAIN):
                chain_copy(c, d).wait_send()
    for d in shifts:
        @pl.when(has(d))
        def _():
            for copy in block_copies(d):
                copy.wait_send()

        @pl.when(has(-d))
        def _():
            for copy in block_copies(d):
                copy.wait_recv()
    for copy in keep:
        copy.wait()


def attend_kernel(
    n, group, hops, docs_ref, q_ref, all_k, all_v, sk_ref, sv_ref, qa_ref, ka_ref,
    o_ref, query, acc,
):
    tile = pl.program_id(1)
    tok = all_k.shape[0] // (2 * hops + 1)
    rows = q_ref.shape[0]
    dim = HEAD_SIZE
    for g in range(group):
        query[g * rows : (g + 1) * rows, :dim] = q_ref[:, g * dim : (g + 1) * dim]
        query[g * rows : (g + 1) * rows, dim:] = qa_ref[...]

    seq_len = n * tok
    first_row = lax.axis_index("seq") * tok
    base = first_row - hops * tok
    a = first_row + tile * rows
    b = a + rows

    def reach(d, carry):
        start, low, high = carry
        end = start + docs_ref[d]
        low = jnp.where(start <= a, start, low)
        high = jnp.where((start < b) & (end >= b), end, high)
        return end, low, high

    _, low, high = lax.fori_loop(
        0, docs_ref.shape[0], reach, (jnp.int32(0), jnp.int32(0), jnp.int32(seq_len))
    )
    low = jnp.maximum(jnp.maximum(low, a - HALF_WIN), jnp.maximum(base, 0)) - base
    high = jnp.minimum(jnp.minimum(high, b + HALF_WIN), jnp.minimum(base + (2 * hops + 1) * tok, seq_len)) - base
    first, last = low // CHUNK, (high + CHUNK - 1) // CHUNK
    sinks = sk_ref.shape[0]
    contract = (((1,), (1,)), ((), ()))

    def sink_scores():
        return lax.dot_general(query[:, :dim], sk_ref[...], contract, preferred_element_type=jnp.float32)

    def chunk_scores(c):
        at = pl.ds(pl.multiple_of(c * CHUNK, CHUNK), CHUNK)
        keys = jnp.concatenate([all_k[at, :], ka_ref[at, :]], axis=1)
        scores = lax.dot_general(query[...], keys, contract, preferred_element_type=jnp.float32)
        if hops > 1:
            i = lax.broadcasted_iota(jnp.int32, (rows, CHUNK), 0) + tile * rows
            j = lax.broadcasted_iota(jnp.int32, (rows, CHUNK), 1) + c * CHUNK - hops * tok
            near = jnp.where(jnp.abs(i - j) <= HALF_WIN, 0.0, HIDE)
            scores = scores + jnp.concatenate([near] * group, axis=0)
        return scores

    def with_ones(values):
        return jnp.concatenate([values, jnp.ones(values.shape, values.dtype)], axis=1)

    def chunk_values(c):
        at = pl.ds(pl.multiple_of(c * CHUNK, CHUNK), CHUNK)
        return with_ones(all_v[at, :])

    def accumulate(weigh):
        acc[...] = jnp.dot(weigh(sink_scores()), with_ones(sv_ref[...]), preferred_element_type=jnp.float32)

        @pl.loop(first, last)
        def _(c):
            acc[...] += jnp.dot(weigh(chunk_scores(c)), chunk_values(c), preferred_element_type=jnp.float32)

    accumulate(lambda s: jnp.exp2(s * EXP2_SCALE).astype(jnp.bfloat16))

    def finish():
        for g in range(group):
            part = acc[g * rows : (g + 1) * rows, :]
            o_ref[:, g * dim : (g + 1) * dim] = (part[:, :dim] / part[:, dim:]).astype(o_ref.dtype)

    total = acc[:, dim:]
    in_range = (jnp.min(total) >= 2.0**-60) & (jnp.max(total) <= 2.0**100)
    finish()

    @pl.when(jnp.logical_not(in_range))
    def _():
        top = jnp.max(sink_scores(), axis=1, keepdims=True)
        top = lax.fori_loop(
            first, last,
            lambda c, m: jnp.maximum(m, jnp.max(chunk_scores(c), axis=1, keepdims=True)),
            top,
        )
        accumulate(lambda s: jnp.exp2((s - top) * EXP2_SCALE).astype(jnp.bfloat16))
        finish()


def on_device(n, queries, keys, values, doc_lengths, sink_rows):
    tok, width = keys.shape
    dim = HEAD_SIZE
    kv_heads = width // dim
    group = queries.shape[1] // width
    seq_len = tok * n
    sinks = sink_rows.shape[0]
    docs = doc_lengths.shape[0]
    longest = seq_len // 4
    hops = min(-(-min(HALF_WIN, longest - 1) // tok), n - 1)
    span = (2 * hops + 1) * tok
    any_space = pl.BlockSpec(memory_space=pl.ANY)
    vmem = pl.BlockSpec(memory_space=pltpu.VMEM)
    bf16 = jnp.bfloat16
    dma = pltpu.SemaphoreType.DMA

    near_k, near_v, sink_k, sink_v, q_side, k_side = pl.pallas_call(
        functools.partial(exchange_kernel, n, hops),
        out_shape=[
            jax.ShapeDtypeStruct((span, width), bf16),
            jax.ShapeDtypeStruct((span, width), bf16),
            jax.ShapeDtypeStruct((sinks, width), bf16),
            jax.ShapeDtypeStruct((sinks, width), bf16),
            jax.ShapeDtypeStruct((tok, dim), bf16),
            jax.ShapeDtypeStruct((span, dim), bf16),
        ],
        in_specs=[vmem] * 5,
        out_specs=[any_space, any_space, vmem, vmem, vmem, vmem],
        scratch_shapes=[pltpu.VMEM((sinks, 2 * width), bf16)] * 5
        + [dma((2 * hops,))] * 4 + [dma((CHAIN,))] * 4 + [dma((2,))],
        compiler_params=pltpu.CompilerParams(
            collective_id=0, has_side_effects=True, vmem_limit_bytes=60 << 20
        ),
        name="exchange",
    )(keys, values, sink_rows.reshape(sinks, 1), sink_rows.reshape(1, sinks), doc_lengths.reshape(docs, 1))

    return pl.pallas_call(
        functools.partial(attend_kernel, n, group, hops),
        out_shape=jax.ShapeDtypeStruct(queries.shape, queries.dtype),
        grid_spec=pltpu.PrefetchScalarGridSpec(
            num_scalar_prefetch=1,
            grid=(kv_heads, tok // TILE),
            in_specs=[
                pl.BlockSpec((TILE, group * dim), lambda h, t, s: (t, h)),
                pl.BlockSpec((span, dim), lambda h, t, s: (0, h)),
                pl.BlockSpec((span, dim), lambda h, t, s: (0, h)),
                pl.BlockSpec((sinks, dim), lambda h, t, s: (0, h)),
                pl.BlockSpec((sinks, dim), lambda h, t, s: (0, h)),
                pl.BlockSpec((TILE, dim), lambda h, t, s: (t, 0)),
                pl.BlockSpec((span, dim), lambda h, t, s: (0, 0)),
            ],
            out_specs=pl.BlockSpec((TILE, group * dim), lambda h, t, s: (t, h)),
            scratch_shapes=[
                pltpu.VMEM((TILE * group, 2 * dim), bf16),
                pltpu.VMEM((TILE * group, 2 * dim), jnp.float32),
            ],
        ),
        compiler_params=pltpu.CompilerParams(vmem_limit_bytes=60 << 20),
        name="attend",
    )(doc_lengths, queries, near_k, near_v, sink_k, sink_v, q_side, k_side)


def solution(mesh):
    return jax.shard_map(
        functools.partial(on_device, mesh.shape["seq"]),
        mesh=mesh,
        in_specs=(
            P(("dp", "seq"), "head"),
            P(("dp", "seq"), "head"),
            P(("dp", "seq"), "head"),
            P("dp"),
            P("dp"),
        ),
        out_specs=P(("dp", "seq"), "head"),
        check_vma=False,
    )
```
